32 devices in a mesh: grp: 4 (over z), orb: 4 (over y, core), slab: 2 (over x).
Axes of the slice: x: 2, y: 2, z: 4, core: 2. Of those that a mesh axis runs over, the one named last changes fastest.
Arguments:
- orbitals: float32 [128, 64, 64, 64], P(('grp', 'orb'), 'slab'), may hold values from -6 to 6
- offsets: int32 [128, 2], replicated, may hold values from 0 to 15
- pairs: int32 [128, 2], P(('grp', 'orb')), may hold values from 0 to 127, as said below
- live: int32 [128], P(('grp', 'orb')), may hold values from 0 to 1, as said below
Outputs:
- exchange: float32 [128, 64, 64, 64], P(('grp', 'orb'), 'slab')
The draws below stay inside these ranges and needn't reach their ends.
Inputs may be any that keep to these rules, and one draw needn't show every extreme that they name: The 8 rows of one device of grp and orb (aligned blocks, in order) name as first orbital one of that device's 8 orbitals; the second orbital lies within 8 positions of the first on the cycle of 128 orbitals. In every block, row 0 pairs the device's lowest orbital with the orbital just below it on the cycle, and row 1 pairs the device's highest orbital with the orbital just above it. In each aligned block of 8 slots the live ones come first, at least two are live, and some block is all live.
All inputs are finite; a program needn't handle non-finite values.
Results may differ from the reference program's by a relative error of at most 0.0003.
Values sent between devices are 32-bit elements; how exact they have to be, the bound alone decides.
A program may use at most 192 MiB of HBM per device.

```python
import jax
import jax.numpy as jnp
from jax import lax

BOX = 64
MAXOFF = 16
PASSES = 8
ORB_DEV = 8
PAIR_DEV = 8
NORB = 128
PAIRS = 128


def draw_pairs(key, part):
    base = jax.random.fold_in(key, 7)
    key_one, key_two = jax.random.split(base)
    owner = jnp.arange(PAIRS, dtype=jnp.int32) // PAIR_DEV
    slot = jnp.arange(PAIRS, dtype=jnp.int32) % PAIR_DEV
    pick = jax.random.randint(key_one, (PAIRS,), 0, ORB_DEV, dtype=jnp.int32)
    pick = jnp.where(slot == 0, 0, jnp.where(slot == 1, ORB_DEV - 1, pick))
    first = owner * ORB_DEV + pick
    step = jax.random.randint(key_two, (PAIRS,), -ORB_DEV, ORB_DEV + 1, dtype=jnp.int32)
    step = jnp.where(slot == 0, -1, jnp.where(slot == 1, 1, step))
    second = jnp.mod(first + step, NORB)
    return jnp.stack([first, second], axis=1).astype(jnp.int32)


def draw_live(key, part):
    base = jax.random.fold_in(key, 11)
    key_one, key_two = jax.random.split(base)
    blocks = PAIRS // PAIR_DEV
    drawn = jax.random.randint(key_one, (blocks,), 0, PAIR_DEV, dtype=jnp.int32)
    counts = jnp.minimum(2 + drawn * drawn // PAIR_DEV, PAIR_DEV)
    fullest = jax.random.randint(key_two, (), 0, blocks, dtype=jnp.int32)
    counts = jnp.where(jnp.arange(blocks, dtype=jnp.int32) == fullest, PAIR_DEV, counts)
    slots = jnp.arange(PAIRS, dtype=jnp.int32) % PAIR_DEV
    return (slots < jnp.repeat(counts, PAIR_DEV)).astype(jnp.int32)


def set_ends(values, stream_key, smallest, largest):
    longest = values.shape.index(max(values.shape))
    spots = []
    for shift in (0, 1):
        where = [jax.random.randint(jax.random.fold_in(stream_key, axis), (), 0, length) for axis, length in enumerate(values.shape)]
        where[longest] = (where[longest] + shift) % values.shape[longest]
        spots.append(tuple(where))
    return values.at[spots[0]].set(smallest).at[spots[1]].set(largest)


def shard_levels(own_key, shape, pieces, low, largest):
    def one(position, blocks):
        heights = jax.random.uniform(jax.random.fold_in(jax.random.fold_in(own_key, 6), position), (blocks,), jnp.float32, low / len(pieces), largest / len(pieces))
        return jnp.repeat(jnp.exp(heights), shape[position] // blocks).reshape((-1,) + (1,) * (len(shape) - position - 1))

    level = one(*pieces[0])
    for cut in pieces[1:]:
        level = level * one(*cut)
    return level


def noise(rng, shape, width, most, pieces=(), kind=jnp.bfloat16):
    entries = width * jax.random.normal(rng, shape, jnp.float32)
    if pieces:
        entries = entries * shard_levels(rng, shape, pieces, -0.22, 0.18)
    return jnp.clip(entries, -most, most).astype(kind)


def setup_inputs(seed: int = 0) -> dict:
    splits = jax.random.split(jax.random.key(seed), 5)
    orbitals = noise(splits[0], (NORB, BOX, BOX, BOX), 1.0, 6.0, ((0, 16), (1, 2)), jnp.float32)
    offsets = set_ends(jax.random.randint(splits[1], (NORB, 2), 0, MAXOFF), jax.random.fold_in(splits[1], 1), 0, MAXOFF - 1).astype(jnp.int32)
    pairs = draw_pairs(jax.random.fold_in(splits[4], 71), 0)
    live = draw_live(jax.random.fold_in(splits[4], 71), 0)
    return {"orbitals": orbitals, "offsets": offsets, "pairs": pairs, "live": live}


DIAG = 6.25
THETA = 1.075
DELTA = 0.925


def place(field, shift_y, shift_z):
    lead = field.ndim - 2
    padded = jnp.pad(field, [(0, 0)] * lead + [(MAXOFF, MAXOFF), (MAXOFF, MAXOFF)])
    zero = jnp.zeros((), jnp.int32)
    starts = [zero] * lead + [(MAXOFF - shift_y).astype(jnp.int32), (MAXOFF - shift_z).astype(jnp.int32)]
    return lax.dynamic_slice(padded, starts, field.shape)


def apply_op(padded):
    core = padded[:, 1:-1]
    wider = jnp.pad(core, ((0, 0), (0, 0), (1, 1), (1, 1)))
    near = padded[:, 2:] + padded[:, :-2]
    near = near + wider[:, :, 2:, 1:-1] + wider[:, :, :-2, 1:-1]
    near = near + wider[:, :, 1:-1, 2:] + wider[:, :, 1:-1, :-2]
    return DIAG * core - near


def smooth(density, widen):
    sigma = THETA / DELTA
    resid = density
    value = jnp.zeros_like(density)
    step = resid / (DIAG * THETA)
    coef = 1.0 / sigma
    for turn in range(PASSES):
        value = value + step
        if turn < PASSES - 1:
            resid = resid - apply_op(widen(step))
            coef_new = 1.0 / (2.0 * sigma - coef)
            step = (coef_new * coef) * step + (2.0 * coef_new / DELTA) * (resid / DIAG)
            coef = coef_new
    return value


def pad_first(field):
    return jnp.pad(field, ((0, 0), (1, 1), (0, 0), (0, 0)))


def reference(orbitals, offsets, pairs, live):
    def one(total, row):
        pair_row, alive = row
        first = pair_row[0]
        second = pair_row[1]
        shift = offsets[second] - offsets[first]
        own = orbitals[first]
        partner = place(orbitals[second], shift[0], shift[1])
        density = (own * partner)[None]
        potential = smooth(density, pad_first)[0]
        weight = alive.astype(jnp.float32)
        to_first = weight * potential * partner
        to_second = weight * place(potential * own, -shift[0], -shift[1])
        total = total.at[first].add(to_first)
        total = total.at[second].add(to_second)
        return total, None

    start = jnp.zeros(orbitals.shape, jnp.float32)
    result, _ = lax.scan(one, start, (pairs, live))
    return result
```

```python
import functools

import jax
import jax.numpy as jnp
from jax import lax
from jax.experimental import pallas as pl
from jax.experimental.pallas import tpu as pltpu
from jax.sharding import PartitionSpec as P

PASSES = 8
DIAG = 6.25
THETA = 1.075
DELTA = 0.925
EDGE = PASSES - 1
PAD = 16
CYCLE = ("grp", "orb")
F32 = jnp.float32


def coefs():
    sigma = THETA / DELTA
    coef = 1.0 / sigma
    out = []
    for _ in range(PASSES - 1):
        new = 1.0 / (2.0 * sigma - coef)
        out.append((new * coef, 2.0 * new / (DELTA * DIAG)))
        coef = new
    return out


def lanes(shape):
    return lax.broadcasted_iota(jnp.int32, shape, len(shape) - 1)


def pack_kernel(src, dst):
    half = dst.shape[1]
    dst[0] = jnp.concatenate([src[0, :half], src[0, half:]], axis=-1)


def pack(orbitals):
    n, x, y, z = orbitals.shape
    return pl.pallas_call(
        pack_kernel,
        grid=(n,),
        in_specs=[pl.BlockSpec((1, x, y, z), lambda i: (i, 0, 0, 0))],
        out_specs=pl.BlockSpec((1, x // 2, y, 2 * z), lambda i: (i, 0, 0, 0)),
        out_shape=jax.ShapeDtypeStruct((n, x // 2, y, 2 * z), F32),
        name="pack",
    )(orbitals)


def copy_kernel(idx, src_a, src_b, dst_a, dst_b):
    dst_a[...] = src_a[...]
    dst_b[...] = src_b[...]


def gather(packed, lists, m):
    _, h, y, w = packed.shape
    blk = (1, h, y, w)
    out = jax.ShapeDtypeStruct((m, h, y, w), F32)
    return pl.pallas_call(
        copy_kernel,
        grid_spec=pltpu.PrefetchScalarGridSpec(
            num_scalar_prefetch=1,
            grid=(m,),
            in_specs=[
                pl.BlockSpec(blk, lambda i, idx: (idx[0, i], 0, 0, 0)),
                pl.BlockSpec(blk, lambda i, idx: (idx[1, i], 0, 0, 0)),
            ],
            out_specs=[pl.BlockSpec(blk, lambda i, idx: (i, 0, 0, 0))] * 2,
        ),
        out_shape=[out, out],
        name="gather",
    )(lists, packed, packed)


def place(value, room, a, b):
    y, w = value.shape[1:]
    z = w // 2
    room[:, PAD : PAD + y, :] = value
    moved = room[:, pl.ds(PAD - a, y), :]
    moved = pltpu.roll(moved, lax.rem(b + w, w), axis=2)
    pos = lanes(moved.shape) % z - b
    return jnp.where((pos >= 0) & (pos < z), moved, 0.0)


def clear_room(room):
    y = room.shape[1] - 2 * PAD
    room[:, :PAD, :] = jnp.zeros((room.shape[0], PAD, room.shape[2]), F32)
    room[:, PAD + y :, :] = jnp.zeros((room.shape[0], PAD, room.shape[2]), F32)


def density_kernel(plan, own, mine, prior, nxt, partner, density, low, high, room):
    p = pl.program_id(0)
    kind = plan[4, p]
    a, b = plan[5, p], plan[6, p]

    @pl.when(p == 0)
    def _():
        clear_room(room)

    def go(src):
        part = place(src[0], room, a, b)
        partner[0] = part
        dens = own[0] * part
        density[0] = dens
        h, y, w = dens.shape
        flat = jnp.concatenate([dens[..., : w // 2], dens[..., w // 2 :]], axis=0)
        top, bot = flat[:EDGE], flat[2 * h - EDGE :]
        low[0] = jnp.concatenate([top[:, : y // 2], top[:, y // 2 :]], axis=-1)
        high[0] = jnp.concatenate([bot[:, : y // 2], bot[:, y // 2 :]], axis=-1)

    for value, src in enumerate((mine, prior, nxt)):
        pl.when(kind == value)(functools.partial(go, src))


def densities(plan, packed, prior, nxt):
    slots = plan.shape[1]
    _, h, y, w = packed.shape
    blk = (1, h, y, w)
    eblk = (1, EDGE, y // 2, w)

    def at(row):
        return pl.BlockSpec(blk, lambda i, plan: (plan[row, i], 0, 0, 0))

    full = jax.ShapeDtypeStruct((slots, h, y, w), F32)
    edge = jax.ShapeDtypeStruct((slots,) + eblk[1:], F32)
    here = lambda i, plan: (i, 0, 0, 0)
    return pl.pallas_call(
        density_kernel,
        grid_spec=pltpu.PrefetchScalarGridSpec(
            num_scalar_prefetch=1,
            grid=(slots,),
            in_specs=[at(0), at(1), at(2), at(3)],
            out_specs=[
                pl.BlockSpec(blk, here),
                pl.BlockSpec(blk, here),
                pl.BlockSpec(eblk, here),
                pl.BlockSpec(eblk, here),
            ],
            scratch_shapes=[pltpu.VMEM((h, y + 2 * PAD, w), F32)],
        ),
        out_shape=[full, full, edge, edge],
        name="density",
    )(plan, packed, packed, prior, nxt)


def solve_kernel(
    plan, ends, density, partner, own, below, above,
    acc, acc_prior, acc_next, resid, step_a, step_b, total, mask, room,
):
    p = pl.program_id(0)
    h, y, w = density.shape[1:]
    z = w // 2
    rows = h + 2 * EDGE

    @pl.when(p == 0)
    def _():
        clear_room(room)
        for ref in (acc, acc_prior, acc_next):
            ref[...] = jnp.zeros(ref.shape, F32)
        for ref in (step_a, step_b):
            ref[:, :8, :] = jnp.zeros((rows, 8, w), F32)
            ref[:, 8 + y :, :] = jnp.zeros((rows, 8, w), F32)
        lane = lanes((1, w))
        first = ends[0] == 0
        last = ends[0] == ends[1] - 1
        for t in range(rows):
            plane = jnp.where(lane < z, t - EDGE, t - EDGE + h)
            outside = ((plane < 0) & first) | ((plane >= 2 * h) & last)
            mask[t] = jnp.where(outside, 0.0, 1.0)

    @pl.when(plan[7, p] > 0)
    def _():
        def unfold(part):
            return jnp.concatenate([part[..., :z], part[..., z:]], axis=1)

        dens = density[0]
        line = jnp.concatenate(
            [unfold(below[0]), dens[..., :z], dens[..., z:], unfold(above[0])], axis=0
        )
        resid[...] = jnp.concatenate([line[:rows], line[h:]], axis=-1)
        step_a[:, 8 : 8 + y, :] = resid[...] * (1.0 / (DIAG * THETA))
        total[...] = step_a[EDGE : EDGE + h, 8 : 8 + y, :]
        lane = lanes((y, w)) % z
        not_low = lane > 0
        not_high = lane < z - 1
        bufs = [step_a, step_b]
        for turn, (keep, gain) in enumerate(coefs()):
            now, then = bufs[turn % 2], bufs[1 - turn % 2]
            core_only = turn == PASSES - 2

            def row(t, now=now, then=then, keep=keep, gain=gain, last=core_only):
                core = now[t, 8 : 8 + y, :]
                near = now[t - 1, 8 : 8 + y, :] + now[t + 1, 8 : 8 + y, :]
                near = near + now[t, 7 : 7 + y, :] + now[t, 9 : 9 + y, :]
                near = near + jnp.where(not_low, pltpu.roll(core, 1, axis=1), 0.0)
                near = near + jnp.where(not_high, pltpu.roll(core, w - 1, axis=1), 0.0)
                left = resid[t] - (DIAG * core - near)
                fresh = (keep * core + gain * left) * mask[t]
                if not last:
                    resid[t] = left
                    then[t, 8 : 8 + y, :] = fresh
                return fresh

            lo, hi = turn + 1, rows - turn - 1

            def outer(t, c):
                row(t)
                return c

            def inner(t, c):
                total[t - EDGE] += row(t)
                return c

            if lo < EDGE:
                lax.fori_loop(lo, EDGE, outer, 0)
                lax.fori_loop(EDGE + h, hi, outer, 0)
            lax.fori_loop(EDGE, EDGE + h, inner, 0)

        pot = total[...]
        acc[plan[0, p]] += pot * partner[0]
        back = place(pot * own[0], room, -plan[5, p], -plan[6, p])
        for value, ref in enumerate((acc, acc_prior, acc_next)):

            @pl.when(plan[4, p] == value)
            def _(ref=ref, value=value):
                ref[plan[1 + value, p]] += back


def solve(plan, ends, density, partner, packed, below, above, m):
    slots = plan.shape[1]
    n, h, y, w = packed.shape
    blk = (1, h, y, w)
    eblk = (1, EDGE, y // 2, w)
    rows = h + 2 * EDGE
    here = lambda i, plan, ends: (i, 0, 0, 0)
    fixed = lambda i, plan, ends: (0, 0, 0, 0)
    shapes = [(n, h, y, w), (m, h, y, w), (m, h, y, w)]
    return pl.pallas_call(
        solve_kernel,
        grid_spec=pltpu.PrefetchScalarGridSpec(
            num_scalar_prefetch=2,
            grid=(slots,),
            in_specs=[
                pl.BlockSpec(blk, here),
                pl.BlockSpec(blk, here),
                pl.BlockSpec(blk, lambda i, plan, ends: (plan[0, i], 0, 0, 0)),
                pl.BlockSpec(eblk, here),
                pl.BlockSpec(eblk, here),
            ],
            out_specs=[pl.BlockSpec(s, fixed) for s in shapes],
            scratch_shapes=[
                pltpu.VMEM((rows, y, w), F32),
                pltpu.VMEM((rows, y + 16, w), F32),
                pltpu.VMEM((rows, y + 16, w), F32),
                pltpu.VMEM((h, y, w), F32),
                pltpu.VMEM((rows, 1, w), F32),
                pltpu.VMEM((h, y + 2 * PAD, w), F32),
            ],
        ),
        out_shape=[jax.ShapeDtypeStruct(s, F32) for s in shapes],
        compiler_params=pltpu.CompilerParams(vmem_limit_bytes=56 * 1024 * 1024),
        name="solve",
    )(plan, ends, density, partner, packed, below, above)


def combine_kernel(back, acc, from_next, from_prior, out):
    k = pl.program_id(0)
    h = acc.shape[1]
    z = acc.shape[3] // 2
    value = acc[0]
    value = value + jnp.where(back[1, k] > 0, from_next[0], 0.0)
    value = value + jnp.where(back[3, k] > 0, from_prior[0], 0.0)
    out[0, :h] = value[:, :, :z]
    out[0, h:] = value[:, :, z:]


def combine(back, acc, from_next, from_prior):
    n, h, y, w = acc.shape
    blk = (1, h, y, w)
    return pl.pallas_call(
        combine_kernel,
        grid_spec=pltpu.PrefetchScalarGridSpec(
            num_scalar_prefetch=1,
            grid=(n,),
            in_specs=[
                pl.BlockSpec(blk, lambda i, back: (i, 0, 0, 0)),
                pl.BlockSpec(blk, lambda i, back: (back[0, i], 0, 0, 0)),
                pl.BlockSpec(blk, lambda i, back: (back[2, i], 0, 0, 0)),
            ],
            out_specs=pl.BlockSpec((1, 2 * h, y, w // 2), lambda i, back: (i, 0, 0, 0)),
        ),
        out_shape=jax.ShapeDtypeStruct((n, 2 * h, y, w // 2), F32),
        name="combine",
    )(back, acc, from_next, from_prior)


def cycle(field, by):
    size = lax.axis_size(CYCLE)
    return lax.ppermute(field, CYCLE, [(i, (i + by) % size) for i in range(size)])


def body(orbitals, offsets, pairs, live):
    n = orbitals.shape[0]
    slots = pairs.shape[0]
    total = offsets.shape[0]
    blocks = total // n
    slabs = lax.axis_size("slab")
    me = lax.axis_index(CYCLE)
    packed = pack(orbitals)

    mine = jnp.concatenate([pairs, live[:, None]], axis=1)
    every = lax.all_gather(mine, CYCLE, axis=0)
    ids = jnp.arange(blocks, dtype=jnp.int32)
    second = every[:, :, 1]
    alive = every[:, :, 2] > 0
    orb = jnp.arange(n, dtype=jnp.int32)
    sides = jnp.stack([(ids - 1) % blocks, (ids + 1) % blocks])
    hit = alive[None] & (second[None] // n == sides[:, :, None])
    need = jnp.any(
        hit[..., None] & (second[None, :, :, None] % n == orb), axis=2
    )
    count = jnp.sum(need.astype(jnp.int32), axis=2)
    most = jnp.max(count)

    after, before = (me + 1) % blocks, (me - 1) % blocks
    flags = jnp.stack(
        [need[0, me], need[1, me], need[0, after], need[1, before]]
    ).astype(jnp.int32)
    spot = jnp.sum(
        flags[:, None, :] * (orb[None, :] < orb[:, None]).astype(jnp.int32)[None], axis=2
    )
    lists = jnp.sum(
        (flags[:, None, :] * (spot[:, None, :] == orb[None, :, None])) * orb, axis=2
    )
    back = jnp.stack(
        [spot[2] * flags[2], flags[2], spot[3] * flags[3], flags[3]]
    )

    i, j, on = pairs[:, 0], pairs[:, 1], live > 0
    owner, local = j // n, j % n
    pick_j = (local[:, None] == orb[None, :]).astype(jnp.int32)
    from_prior = (owner == before) & on
    from_next = (owner == after) & on
    kind = jnp.where(from_prior, 1, jnp.where(from_next, 2, 0))
    where_prior = jnp.sum(pick_j * spot[0][None, :], axis=1) * from_prior
    where_next = jnp.sum(pick_j * spot[1][None, :], axis=1) * from_next
    ids_all = jnp.arange(total, dtype=jnp.int32)
    diff = (j[:, None] == ids_all).astype(jnp.int32) - (i[:, None] == ids_all).astype(jnp.int32)
    shift = jnp.sum(diff[:, :, None] * offsets[None], axis=1)
    plan = jnp.stack(
        [i % n, local, where_prior, where_next, kind, shift[:, 0], shift[:, 1], live]
    ).astype(jnp.int32)
    ends = jnp.stack([lax.axis_index("slab"), slabs]).astype(jnp.int32)

    up = [(s, s + 1) for s in range(slabs - 1)]
    down = [(s + 1, s) for s in range(slabs - 1)]

    def branch(m):
        def run(_):
            to_next, to_prior = gather(packed, lists[2:], m)
            prior = cycle(to_next, 1)
            nxt = cycle(to_prior, -1)
            partner, density, low, high = densities(plan, packed, prior, nxt)
            below = lax.ppermute(high, "slab", up)
            above = lax.ppermute(low, "slab", down)
            acc, acc_prior, acc_next = solve(
                plan, ends, density, partner, packed, below, above, m
            )
            return combine(back, acc, cycle(acc_prior, -1), cycle(acc_next, 1))

        return run

    sizes = sorted({min(s, slots - 1) for s in (2, 3, 4, 5)} | {slots - 1})
    which = sum((most > s).astype(jnp.int32) for s in sizes[:-1])
    return lax.switch(which, [branch(s) for s in sizes], 0)


def solution(mesh):
    placed = (
        P(CYCLE, "slab", None, None),
        P(),
        P(CYCLE, None),
        P(CYCLE),
    )
    return jax.shard_map(
        body,
        mesh=mesh,
        in_specs=placed,
        out_specs=P(CYCLE, "slab", None, None),
        check_vma=False,
    )
```

```python
import functools

import jax
import jax.numpy as jnp
from jax import lax
from jax.experimental import pallas as pl
from jax.experimental.pallas import tpu as pltpu
from jax.sharding import PartitionSpec as P

PASSES = 8
DIAG = 6.25
THETA = 1.075
DELTA = 0.925
EDGE = PASSES - 1
PAD = 16
CYCLE = ("grp", "orb")
F32 = jnp.float32


def coefs():
    sigma = THETA / DELTA
    coef = 1.0 / sigma
    out = []
    for _ in range(PASSES - 1):
        new = 1.0 / (2.0 * sigma - coef)
        out.append((new * coef, 2.0 * new / (DELTA * DIAG)))
        coef = new
    return out


def lanes(shape):
    return lax.broadcasted_iota(jnp.int32, shape, len(shape) - 1)


def share_kernel(mine, every, send_sem, recv_sem):
    size, width = lax.axis_size(CYCLE), lax.axis_size("orb")
    me = lax.axis_index("grp") * width + lax.axis_index("orb")

    def peer(s):
        to = lax.rem(me + s, size)
        return {"grp": lax.div(to, width), "orb": lax.rem(to, width)}

    def greet(s, c):
        pl.semaphore_signal(
            barrier, inc=1, device_id=peer(s), device_id_type=pl.DeviceIdType.MESH
        )
        return c

    def copy(s, slot):
        return pltpu.make_async_remote_copy(
            src_ref=mine,
            dst_ref=every.at[slot],
            send_sem=send_sem.at[s],
            recv_sem=recv_sem.at[s],
            device_id=peer(s),
            device_id_type=pl.DeviceIdType.MESH,
        )

    def send(s, c):
        copy(s, me).start()
        return c

    def finish(s, c):
        copy(s, lax.rem(me + size - s, size)).wait()
        return c

    barrier = pltpu.get_barrier_semaphore()
    lax.fori_loop(1, size, greet, 0)
    pl.semaphore_wait(barrier, size - 1)
    lax.fori_loop(1, size, send, 0)
    every[me] = mine[...]
    lax.fori_loop(1, size, finish, 0)


def share(mine):
    size = lax.axis_size(CYCLE)
    vmem = pl.BlockSpec(memory_space=pltpu.VMEM)
    return pl.pallas_call(
        share_kernel,
        in_specs=[vmem],
        out_specs=vmem,
        out_shape=jax.ShapeDtypeStruct((size,) + mine.shape, mine.dtype),
        scratch_shapes=[pltpu.SemaphoreType.DMA((size,)), pltpu.SemaphoreType.DMA((size,))],
        compiler_params=pltpu.CompilerParams(collective_id=0, has_side_effects=True),
        name="share",
    )(mine)


def pack_kernel(src, dst):
    half = dst.shape[1]
    dst[0] = jnp.concatenate([src[0, :half], src[0, half:]], axis=-1)


def pack(orbitals):
    n, x, y, z = orbitals.shape
    return pl.pallas_call(
        pack_kernel,
        grid=(n,),
        in_specs=[pl.BlockSpec((1, x, y, z), lambda i: (i, 0, 0, 0))],
        out_specs=pl.BlockSpec((1, x // 2, y, 2 * z), lambda i: (i, 0, 0, 0)),
        out_shape=jax.ShapeDtypeStruct((n, x // 2, y, 2 * z), F32),
        name="pack",
    )(orbitals)


def copy_kernel(idx, src_a, src_b, dst_a, dst_b):
    dst_a[...] = src_a[...]
    dst_b[...] = src_b[...]


def gather(packed, lists, m):
    _, h, y, w = packed.shape
    blk = (1, h, y, w)
    out = jax.ShapeDtypeStruct((m, h, y, w), F32)
    return pl.pallas_call(
        copy_kernel,
        grid_spec=pltpu.PrefetchScalarGridSpec(
            num_scalar_prefetch=1,
            grid=(m,),
            in_specs=[
                pl.BlockSpec(blk, lambda i, idx: (idx[0, i], 0, 0, 0)),
                pl.BlockSpec(blk, lambda i, idx: (idx[1, i], 0, 0, 0)),
            ],
            out_specs=[pl.BlockSpec(blk, lambda i, idx: (i, 0, 0, 0))] * 2,
        ),
        out_shape=[out, out],
        name="gather",
    )(lists, packed, packed)


def place(value, room, a, b):
    y, w = value.shape[1:]
    z = w // 2
    room[:, PAD : PAD + y, :] = value
    moved = room[:, pl.ds(PAD - a, y), :]
    moved = pltpu.roll(moved, lax.rem(b + w, w), axis=2)
    pos = lanes(moved.shape) % z - b
    return jnp.where((pos >= 0) & (pos < z), moved, 0.0)


def clear_room(room):
    y = room.shape[1] - 2 * PAD
    room[:, :PAD, :] = jnp.zeros((room.shape[0], PAD, room.shape[2]), F32)
    room[:, PAD + y :, :] = jnp.zeros((room.shape[0], PAD, room.shape[2]), F32)


def density_kernel(plan, own, mine, prior, nxt, partner, density, low, high, room):
    p = pl.program_id(0)
    kind = plan[4, p]
    a, b = plan[5, p], plan[6, p]

    @pl.when(p == 0)
    def _():
        clear_room(room)

    on = plan[7, p] > 0

    def go(src):
        part = place(src[0], room, a, b)
        partner[0] = part
        dens = own[0] * part
        density[0] = dens
        h, y, w = dens.shape
        flat = jnp.concatenate([dens[..., : w // 2], dens[..., w // 2 :]], axis=0)
        top, bot = flat[:EDGE], flat[2 * h - EDGE :]
        low[0] = jnp.concatenate([top[:, : y // 2], top[:, y // 2 :]], axis=-1)
        high[0] = jnp.concatenate([bot[:, : y // 2], bot[:, y // 2 :]], axis=-1)

    for value, src in enumerate((mine, prior, nxt)):
        pl.when(on & (kind == value))(functools.partial(go, src))


def densities(plan, packed, prior, nxt):
    slots = plan.shape[1]
    _, h, y, w = packed.shape
    blk = (1, h, y, w)
    eblk = (1, EDGE, y // 2, w)

    def at(row):
        return pl.BlockSpec(
            blk, lambda i, plan: (plan[row, jnp.minimum(i, plan[8, 1] - 1)], 0, 0, 0)
        )

    full = jax.ShapeDtypeStruct((slots, h, y, w), F32)
    edge = jax.ShapeDtypeStruct((slots,) + eblk[1:], F32)
    here = lambda i, plan: (jnp.minimum(i, plan[8, 1] - 1), 0, 0, 0)
    return pl.pallas_call(
        density_kernel,
        grid_spec=pltpu.PrefetchScalarGridSpec(
            num_scalar_prefetch=1,
            grid=(slots,),
            in_specs=[at(0), at(1), at(2), at(3)],
            out_specs=[
                pl.BlockSpec(blk, here),
                pl.BlockSpec(blk, here),
                pl.BlockSpec(eblk, here),
                pl.BlockSpec(eblk, here),
            ],
            scratch_shapes=[pltpu.VMEM((h, y + 2 * PAD, w), F32)],
        ),
        out_shape=[full, full, edge, edge],
        name="density",
    )(plan, packed, packed, prior, nxt)


def solve_kernel(remote, plan, ends, density, partner, own, below, above, *refs):
    accs, (resid, step_a, step_b, total, mask, room) = refs[:-6], refs[-6:]
    acc = accs[0]
    p = pl.program_id(0)
    h, y, w = density.shape[1:]
    z = w // 2
    rows = h + 2 * EDGE
    group = 4 if h % 4 == 0 else 1

    @pl.when(p == 0)
    def _():
        clear_room(room)
        for ref in accs:
            ref[...] = jnp.zeros(ref.shape, F32)
        for ref in (step_a, step_b):
            ref[:, :8, :] = jnp.zeros((rows, 8, w), F32)
            ref[:, 8 + y :, :] = jnp.zeros((rows, 8, w), F32)
        lane = lanes((1, w))
        first = ends[0] == 0
        last = ends[0] == ends[1] - 1
        for t in range(rows):
            plane = jnp.where(lane < z, t - EDGE, t - EDGE + h)
            outside = ((plane < 0) & first) | ((plane >= 2 * h) & last)
            mask[t] = jnp.where(outside, 0.0, 1.0)

    chosen = (plan[4, p] > 0) if remote else (plan[4, p] == 0)

    @pl.when((plan[7, p] > 0) & chosen)
    def _():
        def unfold(part):
            return jnp.concatenate([part[..., :z], part[..., z:]], axis=1)

        dens = density[0]
        line = jnp.concatenate(
            [unfold(below[0]), dens[..., :z], dens[..., z:], unfold(above[0])], axis=0
        )
        resid[...] = jnp.concatenate([line[:rows], line[h:]], axis=-1)
        step_a[:, 8 : 8 + y, :] = resid[...] * (1.0 / (DIAG * THETA))
        total[...] = step_a[EDGE : EDGE + h, 8 : 8 + y, :]
        lane = lanes((y, w)) % z
        not_low = lane > 0
        not_high = lane < z - 1
        bufs = [step_a, step_b]
        for turn, (keep, gain) in enumerate(coefs()):
            now, then = bufs[turn % 2], bufs[1 - turn % 2]
            core_only = turn == PASSES - 2

            def row(t, now=now, then=then, keep=keep, gain=gain):
                core = now[t, 8 : 8 + y, :]
                near = now[t - 1, 8 : 8 + y, :] + now[t + 1, 8 : 8 + y, :]
                near = near + (now[t, 7 : 7 + y, :] + now[t, 9 : 9 + y, :])
                side = jnp.where(not_low, pltpu.roll(core, 1, axis=1), 0.0)
                side = side + jnp.where(not_high, pltpu.roll(core, w - 1, axis=1), 0.0)
                left = (resid[t] - DIAG * core) + (near + side)
                return left, keep * core + gain * left

            def outer(k, c, row=row, then=then):
                for t in (EDGE - 1 - k, EDGE + h + k):
                    left, fresh = row(t)
                    resid[t] = left
                    then[t, 8 : 8 + y, :] = fresh * mask[t]
                return c

            def inner(k, c, row=row, then=then, last=core_only):
                for g in range(group):
                    t = EDGE + k * group + g
                    left, fresh = row(t)
                    if not last:
                        resid[t] = left
                        then[t, 8 : 8 + y, :] = fresh
                    total[t - EDGE] += fresh
                return c

            if turn + 1 < EDGE:
                lax.fori_loop(0, EDGE - turn - 1, outer, 0)
            lax.fori_loop(0, h // group, inner, 0)

        pot = total[...]
        acc[plan[0, p]] += pot * partner[0]
        back = place(pot * own[0], room, -plan[5, p], -plan[6, p])
        if not remote:
            acc[plan[1, p]] += back
        else:
            for value in (1, 2):

                @pl.when(plan[4, p] == value)
                def _(ref=accs[value], value=value):
                    ref[plan[1 + value, p]] += back


def solve(remote, plan, ends, density, partner, packed, below, above, m):
    slots = plan.shape[1]
    n, h, y, w = packed.shape
    blk = (1, h, y, w)
    eblk = (1, EDGE, y // 2, w)
    rows = h + 2 * EDGE

    def spot(i, plan):
        far = plan[8, 0]
        if remote:
            return jnp.minimum(i, jnp.maximum(far - 1, 0))
        return jnp.clip(i, jnp.minimum(far, plan[8, 1] - 1), plan[8, 1] - 1)

    here = lambda i, plan, ends: (spot(i, plan), 0, 0, 0)
    fixed = lambda i, plan, ends: (0, 0, 0, 0)
    shapes = [(n, h, y, w)] + [(m, h, y, w)] * (2 if remote else 0)
    return pl.pallas_call(
        functools.partial(solve_kernel, remote),
        grid_spec=pltpu.PrefetchScalarGridSpec(
            num_scalar_prefetch=2,
            grid=(slots,),
            in_specs=[
                pl.BlockSpec(blk, here),
                pl.BlockSpec(blk, here),
                pl.BlockSpec(blk, lambda i, plan, ends: (plan[0, spot(i, plan)], 0, 0, 0)),
                pl.BlockSpec(eblk, here),
                pl.BlockSpec(eblk, here),
            ],
            out_specs=[pl.BlockSpec(s, fixed) for s in shapes],
            scratch_shapes=[
                pltpu.VMEM((rows, y, w), F32),
                pltpu.VMEM((rows, y + 16, w), F32),
                pltpu.VMEM((rows, y + 16, w), F32),
                pltpu.VMEM((h, y, w), F32),
                pltpu.VMEM((rows, 1, w), F32),
                pltpu.VMEM((h, y + 2 * PAD, w), F32),
            ],
        ),
        out_shape=[jax.ShapeDtypeStruct(s, F32) for s in shapes],
        compiler_params=pltpu.CompilerParams(vmem_limit_bytes=56 * 1024 * 1024),
        cost_estimate=pl.CostEstimate(
            flops=slots * rows * y * w * 100, bytes_accessed=24 << 20, transcendentals=0
        ),
        name="solve_far" if remote else "solve_near",
    )(plan, ends, density, partner, packed, below, above)


def combine_kernel(back, acc, acc_near, from_next, from_prior, out):
    k = pl.program_id(0)
    h = acc.shape[1]
    z = acc.shape[3] // 2
    value = acc[0] + acc_near[0]
    value = value + jnp.where(back[1, k] > 0, from_next[0], 0.0)
    value = value + jnp.where(back[3, k] > 0, from_prior[0], 0.0)
    out[0, :h] = value[:, :, :z]
    out[0, h:] = value[:, :, z:]


def combine(back, acc, acc_near, from_next, from_prior):
    n, h, y, w = acc.shape
    blk = (1, h, y, w)
    return pl.pallas_call(
        combine_kernel,
        grid_spec=pltpu.PrefetchScalarGridSpec(
            num_scalar_prefetch=1,
            grid=(n,),
            in_specs=[
                pl.BlockSpec(blk, lambda i, back: (i, 0, 0, 0)),
                pl.BlockSpec(blk, lambda i, back: (i, 0, 0, 0)),
                pl.BlockSpec(blk, lambda i, back: (back[0, i], 0, 0, 0)),
                pl.BlockSpec(blk, lambda i, back: (back[2, i], 0, 0, 0)),
            ],
            out_specs=pl.BlockSpec((1, 2 * h, y, w // 2), lambda i, back: (i, 0, 0, 0)),
        ),
        out_shape=jax.ShapeDtypeStruct((n, 2 * h, y, w // 2), F32),
        name="combine",
    )(back, acc, acc_near, from_next, from_prior)


def cycle(field, by):
    size = lax.axis_size(CYCLE)
    return lax.ppermute(field, CYCLE, [(i, (i + by) % size) for i in range(size)])


def body(orbitals, offsets, pairs, live):
    n = orbitals.shape[0]
    slots = pairs.shape[0]
    total = offsets.shape[0]
    blocks = total // n
    slabs = lax.axis_size("slab")
    me = lax.axis_index(CYCLE)
    packed = pack(orbitals)

    mine = jnp.concatenate([pairs, live[:, None]], axis=1)
    every = share(jnp.pad(mine, ((0, 0), (0, 128 - mine.shape[1]))))
    ids = jnp.arange(blocks, dtype=jnp.int32)
    second = every[:, :, 1]
    alive = every[:, :, 2] > 0
    orb = jnp.arange(n, dtype=jnp.int32)
    sides = jnp.stack([(ids - 1) % blocks, (ids + 1) % blocks])
    hit = alive[None] & (second[None] // n == sides[:, :, None])
    need = jnp.any(
        hit[..., None] & (second[None, :, :, None] % n == orb), axis=2
    )
    count = jnp.sum(need.astype(jnp.int32), axis=2)
    most = jnp.max(count)

    after, before = (me + 1) % blocks, (me - 1) % blocks
    flags = jnp.stack(
        [need[0, me], need[1, me], need[0, after], need[1, before]]
    ).astype(jnp.int32)
    spot = jnp.sum(
        flags[:, None, :] * (orb[None, :] < orb[:, None]).astype(jnp.int32)[None], axis=2
    )
    lists = jnp.sum(
        (flags[:, None, :] * (spot[:, None, :] == orb[None, :, None])) * orb, axis=2
    )
    back = jnp.stack(
        [spot[2] * flags[2], flags[2], spot[3] * flags[3], flags[3]]
    )

    i, j, on = pairs[:, 0], pairs[:, 1], live > 0
    owner, local = j // n, j % n
    pick_j = (local[:, None] == orb[None, :]).astype(jnp.int32)
    from_prior = (owner == before) & on
    from_next = (owner == after) & on
    kind = jnp.where(from_prior, 1, jnp.where(from_next, 2, 0))
    where_prior = jnp.sum(pick_j * spot[0][None, :], axis=1) * from_prior
    where_next = jnp.sum(pick_j * spot[1][None, :], axis=1) * from_next
    ids_all = jnp.arange(total, dtype=jnp.int32)
    diff = (j[:, None] == ids_all).astype(jnp.int32) - (i[:, None] == ids_all).astype(jnp.int32)
    shift = jnp.sum(diff[:, :, None] * offsets[None], axis=1)
    plan = jnp.stack(
        [i % n, local, where_prior, where_next, kind, shift[:, 0], shift[:, 1], live]
    ).astype(jnp.int32)
    order = jnp.where(on, jnp.where(kind > 0, 0, 1), 2) * slots + jnp.arange(slots)
    rank = jnp.sum((order[None, :] < order[:, None]).astype(jnp.int32), axis=1)
    move = (rank[:, None] == jnp.arange(slots)[None, :]).astype(jnp.int32)
    plan = jnp.sum(plan[:, :, None] * move[None], axis=1)
    far, lively = jnp.sum((kind > 0).astype(jnp.int32)), jnp.sum(on.astype(jnp.int32))
    tail = jnp.where(jnp.arange(slots) == 0, far, lively)
    plan = jnp.concatenate([plan, tail[None]], axis=0)
    ends = jnp.stack([lax.axis_index("slab"), slabs]).astype(jnp.int32)

    up = [(s, s + 1) for s in range(slabs - 1)]
    down = [(s + 1, s) for s in range(slabs - 1)]

    def branch(m):
        def run(_):
            to_next, to_prior = gather(packed, lists[2:], m)
            prior = cycle(to_next, 1)
            nxt = cycle(to_prior, -1)
            partner, density, low, high = densities(plan, packed, prior, nxt)
            below = lax.ppermute(high, "slab", up)
            above = lax.ppermute(low, "slab", down)
            given = (plan, ends, density, partner, packed, below, above, m)
            acc, acc_prior, acc_next = solve(True, *given)
            from_next, from_prior = cycle(acc_prior, -1), cycle(acc_next, 1)
            (acc_near,) = solve(False, *given)
            return combine(back, acc, acc_near, from_next, from_prior)

        return run

    sizes = sorted({min(s, slots - 1) for s in (3, 4, 5)} | {slots - 1})
    which = sum((most > s).astype(jnp.int32) for s in sizes[:-1])
    return lax.switch(which, [branch(s) for s in sizes], 0)


def solution(mesh):
    placed = (
        P(CYCLE, "slab", None, None),
        P(),
        P(CYCLE, None),
        P(CYCLE),
    )
    return jax.shard_map(
        body,
        mesh=mesh,
        in_specs=placed,
        out_specs=P(CYCLE, "slab", None, None),
        check_vma=False,
    )
```
